32 devices in a mesh: groups: 2 (over x), row: 16 (over z, y, core).
Axes of the slice: x: 2, y: 2, z: 4, core: 2. Of those that a mesh axis runs over, the one named last changes fastest.
Arguments:
- pair_rows: bfloat16 [256, 128, 128], P(('groups', 'row')), parts along dimension 0, may hold values from -6 to 6
- in_gain: float32 [128], replicated, may hold values from 0.1 to 1.9
- w_left: bfloat16 [128, 128], replicated, may hold values from -0.5 to 0.5
- w_left_gate: bfloat16 [128, 128], replicated, may hold values from -0.5 to 0.5
- w_right: bfloat16 [128, 128], replicated, may hold values from -0.5 to 0.5
- w_right_gate: bfloat16 [128, 128], replicated, may hold values from -0.5 to 0.5
- w_gate: bfloat16 [128, 128], replicated, may hold values from -0.5 to 0.5
- w_out: bfloat16 [128, 128], replicated, may hold values from -0.5 to 0.5
- out_gain: float32 [128], replicated, may hold values from 0.1 to 1.9
- valid_len: int32 [2], P('groups'), parts along dimension 0, may hold values from 64 to 128
- window: int32 [2], P('groups'), parts along dimension 0, may hold values from 0 to 7
Outputs:
- update: bfloat16 [256, 16, 128], P(('groups', 'row')), parts along dimension 0
The draws below stay inside these ranges and needn't reach their ends.
There are 2 independent parts, one for each index of `groups`. The reference program is written for one: setup_inputs(seed, part) draws one part's arguments, and reference() takes and returns one part's arrays. A program takes and returns all parts, laid end to end along the dimension named above; an argument that names none is the same for every part. Nothing has to cross between parts.
All inputs are finite; a program needn't handle non-finite values.
Results may differ from the reference program's by a relative error of at most 0.0078.
Values may be sent and summed in bfloat16 or wider, within the bound.
A program may use at most 128 MiB of HBM per device.

```python
import jax
import jax.numpy as jnp
from jax import lax

C = 128
TOKENS = 128


def steps_of(key, shape, shards, smallest, high):
    loudness, own = 1.0, jax.random.fold_in(key, 6)
    for axis_at, shards_of in shards:
        heights = jnp.exp(jax.random.uniform(jax.random.fold_in(own, axis_at), (shards_of,), jnp.float32, smallest / len(shards), high / len(shards)))
        loudness = loudness * jnp.repeat(heights, shape[axis_at] // shards_of).reshape([-1 if axis == axis_at else 1 for axis in range(len(shape))])
    return loudness


def scatter_about(own_key, shape, deviation, most, shards=(), kind=jnp.bfloat16):
    drawn = jax.random.normal(own_key, shape, jnp.float32) * deviation
    if len(shards) > 0:
        drawn = steps_of(own_key, shape, shards, -0.22, 0.18) * drawn
    return jnp.clip(drawn, min=-most, max=most).astype(kind)


def setup_inputs(seed: int = 0, part: int = 0) -> dict:
    seeds = jax.random.split(jax.random.key(seed), 12)
    part_splits = jax.random.split(jax.random.fold_in(seeds[11], part), 12)
    return {
        "pair_rows": scatter_about(part_splits[0], (TOKENS, TOKENS, C), 1.0, 6.0, ((0, 16),)),
        "in_gain": jnp.clip(1.0 + 0.18 * jax.random.normal(seeds[1], (C,), jnp.float32), 0.1, 1.9),
        "w_left": scatter_about(seeds[2], (C, C), C ** -0.5, 0.5),
        "w_left_gate": scatter_about(seeds[3], (C, C), C ** -0.5, 0.5),
        "w_right": scatter_about(seeds[4], (C, C), C ** -0.5, 0.5),
        "w_right_gate": scatter_about(seeds[5], (C, C), C ** -0.5, 0.5),
        "w_gate": scatter_about(seeds[6], (C, C), C ** -0.5, 0.5),
        "w_out": scatter_about(seeds[7], (C, C), C ** -0.5, 0.5),
        "out_gain": jnp.clip(1.0 + 0.18 * jax.random.normal(seeds[8], (C,), jnp.float32), 0.1, 1.9),
        "valid_len": jax.random.randint(part_splits[9], (1,), TOKENS // 2, TOKENS + 1).astype(jnp.int32),
        "window": jax.random.randint(part_splits[10], (1,), 0, 8).astype(jnp.int32),
    }


def layer_norm(values, gain):
    mean_v = lax.optimization_barrier(jnp.mean(values, axis=-1, keepdims=True))
    centered = values - mean_v
    variance_v = lax.optimization_barrier(jnp.mean(centered * centered, axis=-1, keepdims=True))
    return centered * lax.rsqrt(variance_v + 1e-05) * gain

def edge_of(normed_rows, w_value, w_gating, mask_rows):
    channels = normed_rows.shape[-1]
    flat_rows = normed_rows.reshape(-1, channels)
    value_part = jnp.dot(flat_rows, w_value, preferred_element_type=jnp.float32)
    gating = jnp.dot(flat_rows, w_gating, preferred_element_type=jnp.float32)
    return ((jax.nn.sigmoid(gating) * value_part).reshape(normed_rows.shape) * mask_rows).astype(jnp.bfloat16)

def reference(pair_rows, in_gain, w_left, w_left_gate, w_right, w_right_gate, w_gate, w_out, out_gain, valid_len, window):
    tokens_all = pair_rows.shape[0]
    channels = pair_rows.shape[2]
    width_win = tokens_all // 8
    normed = layer_norm(pair_rows.astype(jnp.float32), in_gain).astype(jnp.bfloat16)
    col_live = (jnp.arange(tokens_all, dtype=jnp.int32) < valid_len[0]).astype(jnp.float32)
    live_mask = (col_live[:, None] * col_live[None, :])[:, :, None]
    start_row = (window[0] * width_win).astype(jnp.int32)
    left_edge = edge_of(normed, w_left, w_left_gate, live_mask)
    win_rows = lax.dynamic_slice_in_dim(normed, start_row, width_win, 0)
    win_mask = lax.dynamic_slice_in_dim(live_mask, start_row, width_win, 0)
    right_edge = edge_of(win_rows, w_right, w_right_gate, win_mask)
    gate_in = lax.dynamic_slice_in_dim(normed, start_row, width_win, 1)
    gate_vals = jax.nn.sigmoid(jnp.dot(gate_in.reshape(-1, channels), w_gate, preferred_element_type=jnp.float32))
    gate_vals = gate_vals.reshape(tokens_all, width_win, channels)
    product = jnp.einsum('ikc,jkc->ijc', left_edge.astype(jnp.float32), right_edge.astype(jnp.float32))
    normed_out = layer_norm(product, out_gain).astype(jnp.bfloat16)
    projected = jnp.dot(normed_out.reshape(-1, channels), w_out, preferred_element_type=jnp.float32)
    return (gate_vals * projected.reshape(tokens_all, width_win, channels)).astype(jnp.bfloat16)
```

```python
import functools

import jax
import jax.numpy as jnp
from jax import lax
from jax.experimental import pallas as pl
from jax.experimental.pallas import tpu as pltpu
from jax.sharding import PartitionSpec as P


def layer_norm(values, gain):
    mean_v = jnp.mean(values, axis=-1, keepdims=True)
    centered = values - mean_v
    variance_v = jnp.mean(centered * centered, axis=-1, keepdims=True)
    return centered * lax.rsqrt(variance_v + 1e-05) * gain


def on_device(
    pair_rows,
    in_gain,
    w_left,
    w_left_gate,
    w_right,
    w_right_gate,
    w_gate,
    w_out,
    out_gain,
    valid_len,
    window,
):
    my_index = lax.axis_index("row")
    local_rows, tokens_all, channels = pair_rows.shape
    width_win = tokens_all // 8
    valid_upto = valid_len[0]
    start_block = window[0]
    start_row = start_block * width_win
    row_ids = my_index * local_rows + jnp.arange(local_rows, dtype=jnp.int32)
    row_live = (row_ids < valid_upto).astype(jnp.float32)
    col_live = (jnp.arange(tokens_all, dtype=jnp.int32) < valid_upto).astype(jnp.float32)
    live_mask = (row_live[:, None] * col_live[None, :])[:, :, None]
    normed = layer_norm(pair_rows.astype(jnp.float32), in_gain).astype(jnp.bfloat16)
    flat_rows = normed.reshape(-1, channels)
    joined = jnp.concatenate([w_left, w_left_gate, w_right, w_right_gate], axis=1)
    projected = jnp.dot(flat_rows, joined, preferred_element_type=jnp.float32)
    projected = projected.reshape(local_rows, tokens_all, 4 * channels)
    left_edge = (
        jax.nn.sigmoid(projected[:, :, channels : 2 * channels])
        * projected[:, :, :channels]
        * live_mask
    ).astype(jnp.bfloat16)
    right_edge = (
        jax.nn.sigmoid(projected[:, :, 3 * channels :])
        * projected[:, :, 2 * channels : 3 * channels]
        * live_mask
    ).astype(jnp.bfloat16)
    gate_in = lax.dynamic_slice_in_dim(normed, start_row, width_win, 1)
    gate_vals = jax.nn.sigmoid(
        jnp.dot(gate_in.reshape(-1, channels), w_gate, preferred_element_type=jnp.float32)
    )
    gate_vals = gate_vals.reshape(local_rows, width_win, channels)
    regrouped = lax.all_to_all(right_edge, "row", split_axis=1, concat_axis=0, tiled=True)
    picked = lax.dynamic_slice_in_dim(regrouped, start_row, width_win, 0)
    window_right = lax.all_gather(picked, "row", axis=1, tiled=True)
    product = jnp.einsum(
        "ikc,jkc->ijc", left_edge, window_right, preferred_element_type=jnp.float32
    )
    normed_out = layer_norm(product, out_gain).astype(jnp.bfloat16)
    result = jnp.dot(normed_out.reshape(-1, channels), w_out, preferred_element_type=jnp.float32)
    return (gate_vals * result.reshape(local_rows, width_win, channels)).astype(jnp.bfloat16)


MESH = pl.DeviceIdType.MESH
CHUNKS = 4
LINE = 4
Y1, NEAR, EXCH, FAR, Y2, C1, C2 = range(7)


def fused_kernel(
    valid_ref,
    window_ref,
    x_ref,
    in_gain_ref,
    w_left_ref,
    w_left_gate_ref,
    w_right_ref,
    w_right_gate_ref,
    w_gate_ref,
    w_out_ref,
    out_gain_ref,
    o_ref,
    normed_ref,
    left_ref,
    right_ref,
    from_y,
    here,
    near,
    best,
    other,
    win_ref,
    prod_ref,
    send_sem,
    recv_sem,
):
    local_rows, tokens, channels = x_ref.shape
    half = tokens // 2
    width = o_ref.shape[1]
    step = local_rows // CHUNKS

    me = lax.axis_index("row")
    core = lax.rem(me, 2)
    chip = lax.div(me, 2)
    y = lax.rem(chip, 2)
    z = lax.div(chip, 2)
    zrem = lax.rem(z, 2)
    zhalf = lax.div(z, 2)

    def at(z_, y_, core_):
        return {"row": (z_ * 2 + y_) * 2 + core_}

    y_peer = at(z, 1 - y, core)
    core_peer = at(z, y, 1 - core)
    pair_peer = at(zhalf * 2 + 1 - zrem, y, core)
    inner_peer = at(LINE - 1 - z, y, core)
    outer = jnp.logical_or(z == 0, z == LINE - 1)
    inner = jnp.logical_not(outer)
    mine = pl.ds(pl.multiple_of(y * half, half), half)
    theirs = pl.ds(pl.multiple_of((1 - y) * half, half), half)

    def copy(kind, q):
        rows = pl.ds(q * step, step)
        src, dst, dev = {
            Y1: (right_ref.at[rows, theirs], from_y.at[rows], y_peer),
            NEAR: (here.at[rows], near.at[rows], pair_peer),
            EXCH: (best.at[rows], other.at[rows], inner_peer),
            FAR: (win_ref.at[core, rows, mine], win_ref.at[core, rows, mine], pair_peer),
            Y2: (win_ref.at[core, rows, mine], win_ref.at[core, rows, mine], y_peer),
            C1: (win_ref.at[core, rows, mine], win_ref.at[core, rows, mine], core_peer),
            C2: (win_ref.at[core, rows, theirs], win_ref.at[core, rows, theirs], core_peer),
        }[kind]
        return pltpu.make_async_remote_copy(
            src_ref=src,
            dst_ref=dst,
            send_sem=send_sem.at[kind, q],
            recv_sem=recv_sem.at[kind, q],
            device_id=dev,
            device_id_type=MESH,
        )

    barrier = pltpu.get_barrier_semaphore()
    for peer in (y_peer, core_peer, pair_peer):
        pl.semaphore_signal(barrier, inc=1, device_id=peer, device_id_type=MESH)

    @pl.when(inner)
    def _():
        pl.semaphore_signal(barrier, inc=1, device_id=inner_peer, device_id_type=MESH)
        pl.semaphore_wait(barrier, 4)

    @pl.when(outer)
    def _():
        pl.semaphore_wait(barrier, 3)

    win = window_ref[0]
    win_v = jnp.full((half, channels), win, jnp.int32)

    def flag(cond):
        return jnp.where(cond, 1.0, 0.0).astype(jnp.bfloat16)

    def within(first, count):
        return jnp.logical_and(win_v >= first, win_v < first + count)

    own_y = flag((win_v & 1) == y)
    own_z = flag(within(2 * z, 2))
    own_half = flag(within(4 * zhalf, 4))

    def pick(own, a, b):
        return jnp.where((own > 0)[None], a, b)

    gain = in_gain_ref[...]
    w_r = jnp.concatenate([w_right_ref[...], w_right_gate_ref[...]], axis=1)
    k_ids = lax.broadcasted_iota(jnp.int32, (tokens, channels), 0)
    valid_v = jnp.full((tokens, channels), valid_ref[0], jnp.int32)
    k_live = k_ids < valid_v

    def edge(flat, weights, first, count):
        proj = jnp.dot(flat, weights, preferred_element_type=jnp.float32)
        val = jax.nn.sigmoid(proj[:, channels:]) * proj[:, :channels]
        val = val.reshape(count, tokens, channels)
        out = []
        for r in range(count):
            row_v = jnp.full((tokens, channels), me * local_rows + first + r, jnp.int32)
            live = jnp.logical_and(k_live, row_v < valid_v)
            out.append(jnp.where(live, val[r], 0.0).astype(jnp.bfloat16))
        return out

    for q in range(CHUNKS):
        rows = pl.ds(q * step, step)
        x = x_ref[rows].astype(jnp.float32).reshape(step * tokens, channels)
        normed = layer_norm(x, gain).astype(jnp.bfloat16)
        normed_ref[rows] = normed.reshape(step, tokens, channels)
        for r, e in enumerate(edge(normed, w_r, q * step, step)):
            right_ref[q * step + r] = e
        copy(Y1, q).start()

    def combine_y(q):
        rows = pl.ds(q * step, step)
        copy(Y1, q).wait_recv()
        here[rows] = pick(own_y, right_ref[rows, mine], from_y[rows])

    w_l = jnp.concatenate([w_left_ref[...], w_left_gate_ref[...]], axis=1)

    def left_chunk(q):
        flat = normed_ref[pl.ds(q * step, step)].reshape(step * tokens, channels)
        for r, e in enumerate(edge(flat, w_l, q * step, step)):
            left_ref[q * step + r] = e.astype(jnp.float32)

    for q in range(CHUNKS):
        combine_y(q)

        @pl.when(outer)
        def _():
            copy(NEAR, q).start()

        left_chunk(q)

    @pl.when(inner)
    def _():
        for q in range(CHUNKS):
            rows = pl.ds(q * step, step)
            copy(NEAR, q).wait_recv()
            best[rows] = pick(own_z, here[rows], near[rows])
            copy(EXCH, q).start()

    gate_in = normed_ref[:, :width, :]
    for block in range(1, tokens // width):
        at_block = flag(win_v[:width] == block)
        gate_in = pick(at_block, normed_ref[:, block * width : (block + 1) * width, :], gate_in)
    gate_in = gate_in.reshape(local_rows * width, channels)
    gate_vals = jax.nn.sigmoid(
        jnp.dot(gate_in, w_gate_ref[...], preferred_element_type=jnp.float32)
    )

    for q in range(CHUNKS):
        rows = pl.ds(q * step, step)

        @pl.when(inner)
        def _():
            copy(EXCH, q).wait_recv()
            win_ref[core, rows, mine] = pick(own_half, best[rows], other[rows])
            copy(FAR, q).start()

        @pl.when(outer)
        def _():
            copy(FAR, q).wait_recv()

        copy(Y2, q).start()
        copy(C1, q).start()

    def contract(side, q):
        for r in range(step):
            row = q * step + r
            right = win_ref[side, row].astype(jnp.float32)
            prod_ref[:, pl.ds(side * local_rows + row, 1), :] = jnp.sum(
                left_ref[...] * right[None], axis=1, keepdims=True
            )

    for q in range(CHUNKS + 1):
        if q < CHUNKS:
            copy(Y2, q).wait_recv()
            copy(C2, q).start()
            contract(core, q)
        if q > 0:
            copy(C1, q - 1).wait_recv()
            copy(C2, q - 1).wait_recv()
            contract(1 - core, q - 1)

    product = prod_ref[...].reshape(local_rows * width, channels)
    normed_out = layer_norm(product, out_gain_ref[...]).astype(jnp.bfloat16)
    result = jnp.dot(normed_out, w_out_ref[...], preferred_element_type=jnp.float32)
    o_ref[...] = (gate_vals * result).astype(jnp.bfloat16).reshape(local_rows, width, channels)

    for q in range(CHUNKS):
        for kind in (Y1, Y2, C1, C2):
            copy(kind, q).wait_send()

        @pl.when(outer)
        def _():
            copy(NEAR, q).wait_send()

        @pl.when(inner)
        def _():
            copy(EXCH, q).wait_send()
            copy(FAR, q).wait_send()


def fused(
    pair_rows, in_gain, w_left, w_left_gate, w_right, w_right_gate, w_gate, w_out, out_gain, valid_len, window
):
    local_rows, tokens, channels = pair_rows.shape
    width = tokens // 8
    vmem = pl.BlockSpec(memory_space=pltpu.VMEM)
    smem = pl.BlockSpec(memory_space=pltpu.SMEM)
    part = pltpu.VMEM((local_rows, tokens // 2, channels), jnp.bfloat16)
    return pl.pallas_call(
        fused_kernel,
        out_shape=jax.ShapeDtypeStruct((local_rows, width, channels), jnp.bfloat16),
        in_specs=[smem, smem] + [vmem] * 9,
        out_specs=vmem,
        scratch_shapes=[
            pltpu.VMEM((local_rows, tokens, channels), jnp.bfloat16),
            pltpu.VMEM((local_rows, tokens, channels), jnp.float32),
            pltpu.VMEM((local_rows, tokens, channels), jnp.bfloat16),
            part,
            part,
            part,
            part,
            part,
            pltpu.VMEM((2, local_rows, tokens, channels), jnp.bfloat16),
            pltpu.VMEM((local_rows, width, channels), jnp.float32),
            pltpu.SemaphoreType.DMA((7, CHUNKS)),
            pltpu.SemaphoreType.DMA((7, CHUNKS)),
        ],
        compiler_params=pltpu.CompilerParams(collective_id=0, has_side_effects=True),
    )(
        valid_len,
        window,
        pair_rows,
        in_gain.reshape(1, channels),
        w_left,
        w_left_gate,
        w_right,
        w_right_gate,
        w_gate,
        w_out,
        out_gain.reshape(1, channels),
    )


def on_device_any(row_devices, pair_rows, *rest):
    local_rows, tokens, channels = pair_rows.shape
    fits = row_devices == LINE * 4 and tokens // 8 == 2 * local_rows and local_rows % CHUNKS == 0
    return (fused if fits else on_device)(pair_rows, *rest)


def solution(mesh):
    return jax.shard_map(
        functools.partial(on_device_any, mesh.shape["row"]),
        mesh=mesh,
        in_specs=(
            P(("groups", "row"), None, None),
            P(),
            P(),
            P(),
            P(),
            P(),
            P(),
            P(),
            P(),
            P("groups"),
            P("groups"),
        ),
        out_specs=P(("groups", "row"), None, None),
        check_vma=False,
    )
```

```python
import functools

import jax
import jax.numpy as jnp
from jax import lax
from jax.experimental import pallas as pl
from jax.experimental.pallas import tpu as pltpu
from jax.sharding import PartitionSpec as P


def layer_norm(values, gain):
    mean_v = jnp.mean(values, axis=-1, keepdims=True)
    centered = values - mean_v
    variance_v = jnp.mean(centered * centered, axis=-1, keepdims=True)
    return centered * lax.rsqrt(variance_v + 1e-05) * gain


def on_device(
    pair_rows,
    in_gain,
    w_left,
    w_left_gate,
    w_right,
    w_right_gate,
    w_gate,
    w_out,
    out_gain,
    valid_len,
    window,
):
    my_index = lax.axis_index("row")
    local_rows, tokens_all, channels = pair_rows.shape
    width_win = tokens_all // 8
    valid_upto = valid_len[0]
    start_block = window[0]
    start_row = start_block * width_win
    row_ids = my_index * local_rows + jnp.arange(local_rows, dtype=jnp.int32)
    row_live = (row_ids < valid_upto).astype(jnp.float32)
    col_live = (jnp.arange(tokens_all, dtype=jnp.int32) < valid_upto).astype(jnp.float32)
    live_mask = (row_live[:, None] * col_live[None, :])[:, :, None]
    normed = layer_norm(pair_rows.astype(jnp.float32), in_gain).astype(jnp.bfloat16)
    flat_rows = normed.reshape(-1, channels)
    joined = jnp.concatenate([w_left, w_left_gate, w_right, w_right_gate], axis=1)
    projected = jnp.dot(flat_rows, joined, preferred_element_type=jnp.float32)
    projected = projected.reshape(local_rows, tokens_all, 4 * channels)
    left_edge = (
        jax.nn.sigmoid(projected[:, :, channels : 2 * channels])
        * projected[:, :, :channels]
        * live_mask
    ).astype(jnp.bfloat16)
    right_edge = (
        jax.nn.sigmoid(projected[:, :, 3 * channels :])
        * projected[:, :, 2 * channels : 3 * channels]
        * live_mask
    ).astype(jnp.bfloat16)
    gate_in = lax.dynamic_slice_in_dim(normed, start_row, width_win, 1)
    gate_vals = jax.nn.sigmoid(
        jnp.dot(gate_in.reshape(-1, channels), w_gate, preferred_element_type=jnp.float32)
    )
    gate_vals = gate_vals.reshape(local_rows, width_win, channels)
    regrouped = lax.all_to_all(right_edge, "row", split_axis=1, concat_axis=0, tiled=True)
    picked = lax.dynamic_slice_in_dim(regrouped, start_row, width_win, 0)
    window_right = lax.all_gather(picked, "row", axis=1, tiled=True)
    product = jnp.einsum(
        "ikc,jkc->ijc", left_edge, window_right, preferred_element_type=jnp.float32
    )
    normed_out = layer_norm(product, out_gain).astype(jnp.bfloat16)
    result = jnp.dot(normed_out.reshape(-1, channels), w_out, preferred_element_type=jnp.float32)
    return (gate_vals * result.reshape(local_rows, width_win, channels)).astype(jnp.bfloat16)


MESH = pl.DeviceIdType.MESH
CHUNKS = 2
QUAD = 4
QUARTER, CROSS, GATHER, SWAP = 0, 3, 4, 7


def fused_kernel(
    valid_ref,
    window_ref,
    x_ref,
    in_gain_ref,
    w_left_ref,
    w_left_gate_ref,
    w_right_ref,
    w_right_gate_ref,
    w_gate_ref,
    w_out_ref,
    out_gain_ref,
    o_ref,
    normed_ref,
    left_ref,
    right_ref,
    parts,
    best,
    cross,
    win_ref,
    prod_ref,
    send_sem,
    recv_sem,
):
    local_rows, tokens, channels = x_ref.shape
    depth = tokens // QUAD
    width = o_ref.shape[1]
    step = local_rows // CHUNKS

    me = lax.axis_index("row")
    core = lax.rem(me, 2)
    chip = lax.div(me, 2)
    quad = lax.div(chip, QUAD)
    spot = lax.rem(chip, QUAD)
    y = lax.rem(spot, 2)
    z = lax.div(spot, 2)
    spots = ((1 - z) * 2 + 1 - y, (1 - z) * 2 + y, z * 2 + 1 - y)

    def at(quad_, spot_, core_):
        return {"row": (quad_ * QUAD + spot_) * 2 + core_}

    peers = [at(quad, s, core) for s in spots]
    cross_peer = at(1 - quad, spot, core)
    core_peer = at(quad, spot, 1 - core)

    def quarter(s):
        return pl.ds(pl.multiple_of(s * depth, depth), depth)

    mine = quarter(spot)

    def copy(kind, q):
        rows = pl.ds(q * step, step)
        if kind < CROSS:
            src, dst, dev = right_ref.at[rows, quarter(spots[kind])], parts.at[kind, rows], peers[kind]
        elif kind == CROSS:
            src, dst, dev = best.at[rows], cross.at[rows], cross_peer
        elif kind < SWAP:
            src = dst = win_ref.at[core, rows, mine]
            dev = peers[kind - GATHER]
        else:
            src = dst = win_ref.at[core, rows]
            dev = core_peer
        return pltpu.make_async_remote_copy(
            src_ref=src,
            dst_ref=dst,
            send_sem=send_sem.at[kind, q],
            recv_sem=recv_sem.at[kind, q],
            device_id=dev,
            device_id_type=MESH,
        )

    barrier = pltpu.get_barrier_semaphore()
    everyone = peers + [cross_peer, core_peer]
    for peer in everyone:
        pl.semaphore_signal(barrier, inc=1, device_id=peer, device_id_type=MESH)
    pl.semaphore_wait(barrier, len(everyone))

    win = window_ref[0]
    win_v = jnp.full((depth, channels), win, jnp.int32)

    def flag(cond):
        return jnp.where(cond, 1.0, 0.0).astype(jnp.bfloat16)

    owners = [flag(win_v == quad * QUAD + s) for s in spots]
    own_quad = flag(jnp.logical_and(win_v >= quad * QUAD, win_v < (quad + 1) * QUAD))

    def pick(own, a, b):
        return jnp.where((own > 0)[None], a, b)

    gain = in_gain_ref[...]
    w_r = jnp.concatenate([w_right_ref[...], w_right_gate_ref[...]], axis=1)
    k_ids = lax.broadcasted_iota(jnp.int32, (tokens, channels), 0)
    valid_v = jnp.full((tokens, channels), valid_ref[0], jnp.int32)
    k_live = k_ids < valid_v

    def edge(flat, weights, first, count):
        proj = jnp.dot(flat, weights, preferred_element_type=jnp.float32)
        val = jax.nn.sigmoid(proj[:, channels:]) * proj[:, :channels]
        val = val.reshape(count, tokens, channels)
        out = []
        for r in range(count):
            row_v = jnp.full((tokens, channels), me * local_rows + first + r, jnp.int32)
            live = jnp.logical_and(k_live, row_v < valid_v)
            out.append(jnp.where(live, val[r], 0.0).astype(jnp.bfloat16))
        return out

    for q in range(CHUNKS):
        rows = pl.ds(q * step, step)
        x = x_ref[rows].astype(jnp.float32).reshape(step * tokens, channels)
        normed = layer_norm(x, gain).astype(jnp.bfloat16)
        normed_ref[rows] = normed.reshape(step, tokens, channels)
        for r, e in enumerate(edge(normed, w_r, q * step, step)):
            right_ref[q * step + r] = e
        for t in range(3):
            copy(QUARTER + t, q).start()

    w_l = jnp.concatenate([w_left_ref[...], w_left_gate_ref[...]], axis=1)

    def left_chunk(q):
        flat = normed_ref[pl.ds(q * step, step)].reshape(step * tokens, channels)
        for r, e in enumerate(edge(flat, w_l, q * step, step)):
            left_ref[q * step + r] = e.astype(jnp.float32)

    for q in range(CHUNKS):
        rows = pl.ds(q * step, step)
        held = right_ref[rows, mine]
        for t in range(3):
            copy(QUARTER + t, q).wait_recv()
            held = pick(owners[t], parts[t, rows], held)
        best[rows] = held
        copy(CROSS, q).start()
        left_chunk(q)

    gate_in = normed_ref[:, :width, :]
    for block in range(1, tokens // width):
        at_block = flag(win_v[:width] == block)
        gate_in = pick(at_block, normed_ref[:, block * width : (block + 1) * width, :], gate_in)
    gate_in = gate_in.reshape(local_rows * width, channels)
    gate_vals = jax.nn.sigmoid(
        jnp.dot(gate_in, w_gate_ref[...], preferred_element_type=jnp.float32)
    )

    for q in range(CHUNKS):
        rows = pl.ds(q * step, step)
        copy(CROSS, q).wait_recv()
        win_ref[core, rows, mine] = pick(own_quad, best[rows], cross[rows])
        for t in range(3):
            copy(GATHER + t, q).start()

    def contract(side, q):
        for r in range(step):
            row = q * step + r
            right = win_ref[side, row].astype(jnp.float32)
            prod_ref[:, pl.ds(side * local_rows + row, 1), :] = jnp.sum(
                left_ref[...] * right[None], axis=1, keepdims=True
            )

    for q in range(CHUNKS + 1):
        if q < CHUNKS:
            for t in range(3):
                copy(GATHER + t, q).wait_recv()
            copy(SWAP, q).start()
            contract(core, q)
        if q > 0:
            copy(SWAP, q - 1).wait_recv()
            contract(1 - core, q - 1)

    product = prod_ref[...].reshape(local_rows * width, channels)
    normed_out = layer_norm(product, out_gain_ref[...]).astype(jnp.bfloat16)
    result = jnp.dot(normed_out, w_out_ref[...], preferred_element_type=jnp.float32)
    o_ref[...] = (gate_vals * result).astype(jnp.bfloat16).reshape(local_rows, width, channels)

    for q in range(CHUNKS):
        for kind in range(SWAP + 1):
            copy(kind, q).wait_send()


def fused(
    pair_rows, in_gain, w_left, w_left_gate, w_right, w_right_gate, w_gate, w_out, out_gain, valid_len, window
):
    local_rows, tokens, channels = pair_rows.shape
    width = tokens // 8
    vmem = pl.BlockSpec(memory_space=pltpu.VMEM)
    smem = pl.BlockSpec(memory_space=pltpu.SMEM)
    part = (local_rows, tokens // QUAD, channels)
    return pl.pallas_call(
        fused_kernel,
        out_shape=jax.ShapeDtypeStruct((local_rows, width, channels), jnp.bfloat16),
        in_specs=[smem, smem] + [vmem] * 9,
        out_specs=vmem,
        scratch_shapes=[
            pltpu.VMEM((local_rows, tokens, channels), jnp.bfloat16),
            pltpu.VMEM((local_rows, tokens, channels), jnp.float32),
            pltpu.VMEM((local_rows, tokens, channels), jnp.bfloat16),
            pltpu.VMEM((3, *part), jnp.bfloat16),
            pltpu.VMEM(part, jnp.bfloat16),
            pltpu.VMEM(part, jnp.bfloat16),
            pltpu.VMEM((2, local_rows, tokens, channels), jnp.bfloat16),
            pltpu.VMEM((local_rows, width, channels), jnp.float32),
            pltpu.SemaphoreType.DMA((SWAP + 1, CHUNKS)),
            pltpu.SemaphoreType.DMA((SWAP + 1, CHUNKS)),
        ],
        compiler_params=pltpu.CompilerParams(collective_id=0, has_side_effects=True),
    )(
        valid_len,
        window,
        pair_rows,
        in_gain.reshape(1, channels),
        w_left,
        w_left_gate,
        w_right,
        w_right_gate,
        w_gate,
        w_out,
        out_gain.reshape(1, channels),
    )


def on_device_any(row_devices, pair_rows, *rest):
    local_rows, tokens, channels = pair_rows.shape
    fits = row_devices == QUAD * 4 and tokens // 8 == 2 * local_rows and local_rows % CHUNKS == 0
    return (fused if fits else on_device)(pair_rows, *rest)


def solution(mesh):
    return jax.shard_map(
        functools.partial(on_device_any, mesh.shape["row"]),
        mesh=mesh,
        in_specs=(
            P(("groups", "row"), None, None),
            P(),
            P(),
            P(),
            P(),
            P(),
            P(),
            P(),
            P(),
            P("groups"),
            P("groups"),
        ),
        out_specs=P(("groups", "row"), None, None),
        check_vma=False,
    )
```

```python
import functools

import jax
import jax.numpy as jnp
from jax import lax
from jax.experimental import pallas as pl
from jax.experimental.pallas import tpu as pltpu
from jax.sharding import PartitionSpec as P


def layer_norm(values, gain):
    mean_v = jnp.mean(values, axis=-1, keepdims=True)
    centered = values - mean_v
    variance_v = jnp.mean(centered * centered, axis=-1, keepdims=True)
    return centered * lax.rsqrt(variance_v + 1e-05) * gain


def on_device(
    pair_rows,
    in_gain,
    w_left,
    w_left_gate,
    w_right,
    w_right_gate,
    w_gate,
    w_out,
    out_gain,
    valid_len,
    window,
):
    my_index = lax.axis_index("row")
    local_rows, tokens_all, channels = pair_rows.shape
    width_win = tokens_all // 8
    valid_upto = valid_len[0]
    start_block = window[0]
    start_row = start_block * width_win
    row_ids = my_index * local_rows + jnp.arange(local_rows, dtype=jnp.int32)
    row_live = (row_ids < valid_upto).astype(jnp.float32)
    col_live = (jnp.arange(tokens_all, dtype=jnp.int32) < valid_upto).astype(jnp.float32)
    live_mask = (row_live[:, None] * col_live[None, :])[:, :, None]
    normed = layer_norm(pair_rows.astype(jnp.float32), in_gain).astype(jnp.bfloat16)
    flat_rows = normed.reshape(-1, channels)
    joined = jnp.concatenate([w_left, w_left_gate, w_right, w_right_gate], axis=1)
    projected = jnp.dot(flat_rows, joined, preferred_element_type=jnp.float32)
    projected = projected.reshape(local_rows, tokens_all, 4 * channels)
    left_edge = (
        jax.nn.sigmoid(projected[:, :, channels : 2 * channels])
        * projected[:, :, :channels]
        * live_mask
    ).astype(jnp.bfloat16)
    right_edge = (
        jax.nn.sigmoid(projected[:, :, 3 * channels :])
        * projected[:, :, 2 * channels : 3 * channels]
        * live_mask
    ).astype(jnp.bfloat16)
    gate_in = lax.dynamic_slice_in_dim(normed, start_row, width_win, 1)
    gate_vals = jax.nn.sigmoid(
        jnp.dot(gate_in.reshape(-1, channels), w_gate, preferred_element_type=jnp.float32)
    )
    gate_vals = gate_vals.reshape(local_rows, width_win, channels)
    regrouped = lax.all_to_all(right_edge, "row", split_axis=1, concat_axis=0, tiled=True)
    picked = lax.dynamic_slice_in_dim(regrouped, start_row, width_win, 0)
    window_right = lax.all_gather(picked, "row", axis=1, tiled=True)
    product = jnp.einsum(
        "ikc,jkc->ijc", left_edge, window_right, preferred_element_type=jnp.float32
    )
    normed_out = layer_norm(product, out_gain).astype(jnp.bfloat16)
    result = jnp.dot(normed_out.reshape(-1, channels), w_out, preferred_element_type=jnp.float32)
    return (gate_vals * result.reshape(local_rows, width_win, channels)).astype(jnp.bfloat16)


MESH = pl.DeviceIdType.MESH
CHUNKS = 2
QUAD = 4
QUARTER, CROSS, GATHER, SWAP = 0, 3, 4, 7


def fused_kernel(
    valid_ref,
    window_ref,
    x_hbm,
    in_gain_hbm,
    w_left_hbm,
    w_left_gate_hbm,
    w_right_hbm,
    w_right_gate_hbm,
    w_gate_hbm,
    w_out_hbm,
    out_gain_hbm,
    o_ref,
    x_ref,
    in_gain_ref,
    w_left_ref,
    w_left_gate_ref,
    w_right_ref,
    w_right_gate_ref,
    w_gate_ref,
    w_out_ref,
    out_gain_ref,
    normed_ref,
    left_ref,
    parts,
    best,
    cross,
    win_ref,
    prod_ref,
    send_sem,
    recv_sem,
    load_sem,
):
    local_rows, tokens, channels = x_ref.shape
    depth = tokens // QUAD
    width = o_ref.shape[1]
    step = local_rows // CHUNKS

    me = lax.axis_index("row")
    core = lax.rem(me, 2)
    chip = lax.div(me, 2)
    quad = lax.div(chip, QUAD)
    spot = lax.rem(chip, QUAD)
    y = lax.rem(spot, 2)
    z = lax.div(spot, 2)
    spots = ((1 - z) * 2 + 1 - y, (1 - z) * 2 + y, z * 2 + 1 - y)

    def at(quad_, spot_, core_):
        return {"row": (quad_ * QUAD + spot_) * 2 + core_}

    peers = [at(quad, s, core) for s in spots]
    cross_peer = at(1 - quad, spot, core)
    core_peer = at(quad, spot, 1 - core)

    def quarter(s):
        return pl.ds(pl.multiple_of(s * depth, depth), depth)

    mine = quarter(spot)

    def copy(kind, q):
        rows = pl.ds(q * step, step)
        if kind < CROSS:
            src, dst, dev = x_hbm.at[rows, quarter(spots[kind])], parts.at[kind, rows], peers[kind]
        elif kind == CROSS:
            src, dst, dev = best.at[rows], cross.at[rows], cross_peer
        elif kind < SWAP:
            src = dst = win_ref.at[core, rows, mine]
            dev = peers[kind - GATHER]
        else:
            src = dst = win_ref.at[core, rows]
            dev = core_peer
        return pltpu.make_async_remote_copy(
            src_ref=src,
            dst_ref=dst,
            send_sem=send_sem.at[kind, q],
            recv_sem=recv_sem.at[kind, q],
            device_id=dev,
            device_id_type=MESH,
        )

    barrier = pltpu.get_barrier_semaphore()
    everyone = peers + [cross_peer, core_peer]
    for peer in everyone:
        pl.semaphore_signal(barrier, inc=1, device_id=peer, device_id_type=MESH)
    loads = [
        pltpu.make_async_copy(src, dst, load_sem.at[n])
        for n, (src, dst) in enumerate(
            (
                (x_hbm, x_ref),
                (in_gain_hbm, in_gain_ref),
                (w_left_hbm, w_left_ref),
                (w_left_gate_hbm, w_left_gate_ref),
                (w_gate_hbm, w_gate_ref),
                (w_right_hbm, w_right_ref),
                (w_right_gate_hbm, w_right_gate_ref),
                (w_out_hbm, w_out_ref),
                (out_gain_hbm, out_gain_ref),
            )
        )
    ]
    for load in loads:
        load.start()
    pl.semaphore_wait(barrier, len(everyone))
    for q in range(CHUNKS):
        for t in range(3):
            copy(QUARTER + t, q).start()
    for load in loads:
        load.wait()

    win = window_ref[0]
    win_v = jnp.full((depth, channels), win, jnp.int32)

    def flag(cond):
        return jnp.where(cond, 1.0, 0.0).astype(jnp.bfloat16)

    owners = [flag(win_v == quad * QUAD + s) for s in spots]
    own_quad = flag(jnp.logical_and(win_v >= quad * QUAD, win_v < (quad + 1) * QUAD))

    def pick(own, a, b):
        return jnp.where((own > 0)[None], a, b)

    gain = in_gain_ref[...]
    w_r = jnp.concatenate([w_right_ref[...], w_right_gate_ref[...]], axis=1)
    k_ids = lax.broadcasted_iota(jnp.int32, (tokens, channels), 0)
    valid_v = jnp.full((tokens, channels), valid_ref[0], jnp.int32)
    k_live = k_ids < valid_v

    def normal(rows):
        flat = rows.astype(jnp.float32).reshape(step * tokens, channels)
        return layer_norm(flat, gain).astype(jnp.bfloat16)

    def edge(flat, weights, row_v):
        proj = jnp.dot(flat, weights, preferred_element_type=jnp.float32)
        val = jax.nn.sigmoid(proj[:, channels:]) * proj[:, :channels]
        val = val.reshape(step, tokens, channels)
        out = []
        for r in range(step):
            live = jnp.logical_and(k_live, row_v + r < valid_v)
            rounded = jnp.where(live, val[r], 0.0).astype(jnp.bfloat16)
            out.append(rounded.astype(jnp.float32))
        return out

    w_l = jnp.concatenate([w_left_ref[...], w_left_gate_ref[...]], axis=1)

    def left_chunk(q):
        rows = pl.ds(q * step, step)
        flat = normal(x_ref[rows])
        normed_ref[rows] = flat.reshape(step, tokens, channels)
        row_v = jnp.full((tokens, channels), me * local_rows + q * step, jnp.int32)
        for r, e in enumerate(edge(flat, w_l, row_v)):
            left_ref[q * step + r] = e

    for q in range(CHUNKS):
        left_chunk(q)

    gate_in = normed_ref[:, :width, :]
    for block in range(1, tokens // width):
        at_block = flag(win_v[:width] == block)
        gate_in = pick(at_block, normed_ref[:, block * width : (block + 1) * width, :], gate_in)
    gate_in = gate_in.reshape(local_rows * width, channels)
    gate_vals = jax.nn.sigmoid(
        jnp.dot(gate_in, w_gate_ref[...], preferred_element_type=jnp.float32)
    )

    for q in range(CHUNKS):
        rows = pl.ds(q * step, step)
        held = x_ref[rows, mine]
        for t in range(3):
            copy(QUARTER + t, q).wait_recv()
            held = pick(owners[t], parts[t, rows], held)
        best[rows] = held
        copy(CROSS, q).start()

    for q in range(CHUNKS):
        rows = pl.ds(q * step, step)
        copy(CROSS, q).wait_recv()
        win_ref[core, rows, mine] = pick(own_quad, best[rows], cross[rows])
        for t in range(3):
            copy(GATHER + t, q).start()

    def contract(side, q):
        first = side * local_rows + q * step
        row_v = jnp.full((tokens, channels), win * width + first, jnp.int32)
        flat = normal(win_ref[side, pl.ds(q * step, step)])
        for r, right in enumerate(edge(flat, w_r, row_v)):
            prod_ref[:, pl.ds(first + r, 1), :] = jnp.sum(
                left_ref[...] * right[None], axis=1, keepdims=True
            )

    for q in range(CHUNKS + 1):
        if q < CHUNKS:
            for t in range(3):
                copy(GATHER + t, q).wait_recv()
            copy(SWAP, q).start()
            contract(core, q)
        if q > 0:
            copy(SWAP, q - 1).wait_recv()
            contract(1 - core, q - 1)

    product = prod_ref[...].reshape(local_rows * width, channels)
    normed_out = layer_norm(product, out_gain_ref[...]).astype(jnp.bfloat16)
    result = jnp.dot(normed_out, w_out_ref[...], preferred_element_type=jnp.float32)
    o_ref[...] = (gate_vals * result).astype(jnp.bfloat16).reshape(local_rows, width, channels)

    for q in range(CHUNKS):
        for kind in range(SWAP + 1):
            copy(kind, q).wait_send()


def fused(
    pair_rows, in_gain, w_left, w_left_gate, w_right, w_right_gate, w_gate, w_out, out_gain, valid_len, window
):
    local_rows, tokens, channels = pair_rows.shape
    width = tokens // 8
    vmem = pl.BlockSpec(memory_space=pltpu.VMEM)
    smem = pl.BlockSpec(memory_space=pltpu.SMEM)
    part = (local_rows, tokens // QUAD, channels)
    return pl.pallas_call(
        fused_kernel,
        out_shape=jax.ShapeDtypeStruct((local_rows, width, channels), jnp.bfloat16),
        in_specs=[smem, smem] + [pl.BlockSpec(memory_space=pl.ANY)] * 9,
        out_specs=vmem,
        scratch_shapes=[
            pltpu.VMEM((local_rows, tokens, channels), jnp.bfloat16),
            pltpu.VMEM((1, channels), jnp.float32),
            *[pltpu.VMEM((channels, channels), jnp.bfloat16)] * 6,
            pltpu.VMEM((1, channels), jnp.float32),
            pltpu.VMEM((local_rows, tokens, channels), jnp.bfloat16),
            pltpu.VMEM((local_rows, tokens, channels), jnp.float32),
            pltpu.VMEM((3, *part), jnp.bfloat16),
            pltpu.VMEM(part, jnp.bfloat16),
            pltpu.VMEM(part, jnp.bfloat16),
            pltpu.VMEM((2, local_rows, tokens, channels), jnp.bfloat16),
            pltpu.VMEM((local_rows, width, channels), jnp.float32),
            pltpu.SemaphoreType.DMA((SWAP + 1, CHUNKS)),
            pltpu.SemaphoreType.DMA((SWAP + 1, CHUNKS)),
            pltpu.SemaphoreType.DMA((9,)),
        ],
        compiler_params=pltpu.CompilerParams(collective_id=0, has_side_effects=True),
    )(
        valid_len,
        window,
        pair_rows,
        in_gain.reshape(1, channels),
        w_left,
        w_left_gate,
        w_right,
        w_right_gate,
        w_gate,
        w_out,
        out_gain.reshape(1, channels),
    )


def on_device_any(row_devices, pair_rows, *rest):
    local_rows, tokens, channels = pair_rows.shape
    fits = row_devices == QUAD * 4 and tokens // 8 == 2 * local_rows and local_rows % CHUNKS == 0
    return (fused if fits else on_device)(pair_rows, *rest)


def solution(mesh):
    return jax.shard_map(
        functools.partial(on_device_any, mesh.shape["row"]),
        mesh=mesh,
        in_specs=(
            P(("groups", "row"), None, None),
            P(),
            P(),
            P(),
            P(),
            P(),
            P(),
            P(),
            P(),
            P("groups"),
            P("groups"),
        ),
        out_specs=P(("groups", "row"), None, None),
        check_vma=False,
    )
```

```python
import functools

import jax
import jax.numpy as jnp
from jax import lax
from jax.experimental import pallas as pl
from jax.experimental.pallas import tpu as pltpu
from jax.sharding import PartitionSpec as P


def layer_norm(values, gain):
    mean_v = jnp.mean(values, axis=-1, keepdims=True)
    centered = values - mean_v
    variance_v = jnp.mean(centered * centered, axis=-1, keepdims=True)
    return centered * lax.rsqrt(variance_v + 1e-05) * gain


def on_device(
    pair_rows,
    in_gain,
    w_left,
    w_left_gate,
    w_right,
    w_right_gate,
    w_gate,
    w_out,
    out_gain,
    valid_len,
    window,
):
    my_index = lax.axis_index("row")
    local_rows, tokens_all, channels = pair_rows.shape
    width_win = tokens_all // 8
    valid_upto = valid_len[0]
    start_block = window[0]
    start_row = start_block * width_win
    row_ids = my_index * local_rows + jnp.arange(local_rows, dtype=jnp.int32)
    row_live = (row_ids < valid_upto).astype(jnp.float32)
    col_live = (jnp.arange(tokens_all, dtype=jnp.int32) < valid_upto).astype(jnp.float32)
    live_mask = (row_live[:, None] * col_live[None, :])[:, :, None]
    normed = layer_norm(pair_rows.astype(jnp.float32), in_gain).astype(jnp.bfloat16)
    flat_rows = normed.reshape(-1, channels)
    joined = jnp.concatenate([w_left, w_left_gate, w_right, w_right_gate], axis=1)
    projected = jnp.dot(flat_rows, joined, preferred_element_type=jnp.float32)
    projected = projected.reshape(local_rows, tokens_all, 4 * channels)
    left_edge = (
        jax.nn.sigmoid(projected[:, :, channels : 2 * channels])
        * projected[:, :, :channels]
        * live_mask
    ).astype(jnp.bfloat16)
    right_edge = (
        jax.nn.sigmoid(projected[:, :, 3 * channels :])
        * projected[:, :, 2 * channels : 3 * channels]
        * live_mask
    ).astype(jnp.bfloat16)
    gate_in = lax.dynamic_slice_in_dim(normed, start_row, width_win, 1)
    gate_vals = jax.nn.sigmoid(
        jnp.dot(gate_in.reshape(-1, channels), w_gate, preferred_element_type=jnp.float32)
    )
    gate_vals = gate_vals.reshape(local_rows, width_win, channels)
    regrouped = lax.all_to_all(right_edge, "row", split_axis=1, concat_axis=0, tiled=True)
    picked = lax.dynamic_slice_in_dim(regrouped, start_row, width_win, 0)
    window_right = lax.all_gather(picked, "row", axis=1, tiled=True)
    product = jnp.einsum(
        "ikc,jkc->ijc", left_edge, window_right, preferred_element_type=jnp.float32
    )
    normed_out = layer_norm(product, out_gain).astype(jnp.bfloat16)
    result = jnp.dot(normed_out.reshape(-1, channels), w_out, preferred_element_type=jnp.float32)
    return (gate_vals * result.reshape(local_rows, width_win, channels)).astype(jnp.bfloat16)


MESH = pl.DeviceIdType.MESH
CHUNKS = 2
QUAD = 4
QUARTER, CROSS, GATHER, SWAP = 0, 3, 4, 7


def fused_kernel(
    valid_ref,
    window_ref,
    x_hbm,
    in_gain_hbm,
    w_left_hbm,
    w_left_gate_hbm,
    w_right_hbm,
    w_right_gate_hbm,
    w_gate_hbm,
    w_out_hbm,
    out_gain_hbm,
    o_ref,
    x_ref,
    in_gain_ref,
    w_left_ref,
    w_left_gate_ref,
    w_right_ref,
    w_right_gate_ref,
    w_gate_ref,
    w_out_ref,
    out_gain_ref,
    normed_ref,
    left_ref,
    parts,
    best,
    cross,
    win_ref,
    prod_ref,
    send_sem,
    recv_sem,
    load_sem,
):
    local_rows, tokens, channels = x_ref.shape
    depth = tokens // QUAD
    width = o_ref.shape[1]
    step = local_rows // CHUNKS

    me = lax.axis_index("row")
    core = lax.rem(me, 2)
    chip = lax.div(me, 2)
    quad = lax.div(chip, QUAD)
    spot = lax.rem(chip, QUAD)
    y = lax.rem(spot, 2)
    z = lax.div(spot, 2)
    spots = ((1 - z) * 2 + 1 - y, (1 - z) * 2 + y, z * 2 + 1 - y)

    def at(quad_, spot_, core_):
        return {"row": (quad_ * QUAD + spot_) * 2 + core_}

    peers = [at(quad, s, core) for s in spots]
    cross_peer = at(1 - quad, spot, core)
    core_peer = at(quad, spot, 1 - core)

    def quarter(s):
        return pl.ds(pl.multiple_of(s * depth, depth), depth)

    mine = quarter(spot)

    def copy(kind, q):
        rows = pl.ds(q * step, step)
        if kind < CROSS:
            src, dst, dev = x_ref.at[rows, quarter(spots[kind])], parts.at[kind, rows], peers[kind]
        elif kind == CROSS:
            src, dst, dev = best.at[rows], cross.at[rows], cross_peer
        elif kind < SWAP:
            src = dst = win_ref.at[core, rows, mine]
            dev = peers[kind - GATHER]
        else:
            src = dst = win_ref.at[core, rows]
            dev = core_peer
        return pltpu.make_async_remote_copy(
            src_ref=src,
            dst_ref=dst,
            send_sem=send_sem.at[kind, q],
            recv_sem=recv_sem.at[kind, q],
            device_id=dev,
            device_id_type=MESH,
        )

    barrier = pltpu.get_barrier_semaphore()
    everyone = peers + [cross_peer, core_peer]
    for peer in everyone:
        pl.semaphore_signal(barrier, inc=1, device_id=peer, device_id_type=MESH)
    loads = [
        pltpu.make_async_copy(src, dst, load_sem.at[n])
        for n, (src, dst) in enumerate(
            (
                *((x_hbm.at[pl.ds(q * step, step)], x_ref.at[pl.ds(q * step, step)]) for q in range(CHUNKS)),
                (in_gain_hbm, in_gain_ref),
                (w_left_hbm, w_left_ref),
                (w_left_gate_hbm, w_left_gate_ref),
                (w_gate_hbm, w_gate_ref),
                (w_right_hbm, w_right_ref),
                (w_right_gate_hbm, w_right_gate_ref),
                (w_out_hbm, w_out_ref),
                (out_gain_hbm, out_gain_ref),
            )
        )
    ]
    for load in loads:
        load.start()
    pl.semaphore_wait(barrier, len(everyone))
    for q in range(CHUNKS):
        loads[q].wait()
        for t in range(3):
            copy(QUARTER + t, q).start()
    for load in loads[CHUNKS:]:
        load.wait()

    win = window_ref[0]
    win_v = jnp.full((depth, channels), win, jnp.int32)

    def flag(cond):
        return jnp.where(cond, 1.0, 0.0).astype(jnp.bfloat16)

    owners = [flag(win_v == quad * QUAD + s) for s in spots]
    own_quad = flag(jnp.logical_and(win_v >= quad * QUAD, win_v < (quad + 1) * QUAD))

    def pick(own, a, b):
        return jnp.where((own > 0)[None], a, b)

    gain = in_gain_ref[...]
    w_r = jnp.concatenate([w_right_ref[...], w_right_gate_ref[...]], axis=1)
    k_ids = lax.broadcasted_iota(jnp.int32, (tokens, channels), 0)
    valid_v = jnp.full((tokens, channels), valid_ref[0], jnp.int32)
    k_live = k_ids < valid_v

    def normal(rows):
        flat = rows.astype(jnp.float32).reshape(step * tokens, channels)
        return layer_norm(flat, gain).astype(jnp.bfloat16)

    def edge(flat, weights, row_v):
        proj = jnp.dot(flat, weights, preferred_element_type=jnp.float32)
        val = jax.nn.sigmoid(proj[:, channels:]) * proj[:, :channels]
        val = val.reshape(step, tokens, channels)
        out = []
        for r in range(step):
            live = jnp.logical_and(k_live, row_v + r < valid_v)
            rounded = jnp.where(live, val[r], 0.0).astype(jnp.bfloat16)
            out.append(rounded.astype(jnp.float32))
        return out

    w_l = jnp.concatenate([w_left_ref[...], w_left_gate_ref[...]], axis=1)

    def left_chunk(q):
        rows = pl.ds(q * step, step)
        flat = normal(x_ref[rows])
        normed_ref[rows] = flat.reshape(step, tokens, channels)
        row_v = jnp.full((tokens, channels), me * local_rows + q * step, jnp.int32)
        for r, e in enumerate(edge(flat, w_l, row_v)):
            left_ref[q * step + r] = e

    for q in range(CHUNKS):
        left_chunk(q)

    gate_in = normed_ref[:, :width, :]
    for block in range(1, tokens // width):
        at_block = flag(win_v[:width] == block)
        gate_in = pick(at_block, normed_ref[:, block * width : (block + 1) * width, :], gate_in)
    gate_in = gate_in.reshape(local_rows * width, channels)
    gate_vals = jax.nn.sigmoid(
        jnp.dot(gate_in, w_gate_ref[...], preferred_element_type=jnp.float32)
    )

    for q in range(CHUNKS):
        rows = pl.ds(q * step, step)
        held = x_ref[rows, mine]
        for t in range(3):
            copy(QUARTER + t, q).wait_recv()
            held = pick(owners[t], parts[t, rows], held)
        best[rows] = held
        copy(CROSS, q).start()

    for q in range(CHUNKS):
        rows = pl.ds(q * step, step)
        copy(CROSS, q).wait_recv()
        win_ref[core, rows, mine] = pick(own_quad, best[rows], cross[rows])
        for t in range(3):
            copy(GATHER + t, q).start()

    def contract(side, q):
        first = side * local_rows + q * step
        row_v = jnp.full((tokens, channels), win * width + first, jnp.int32)
        flat = normal(win_ref[side, pl.ds(q * step, step)])
        for r, right in enumerate(edge(flat, w_r, row_v)):
            prod_ref[:, pl.ds(first + r, 1), :] = jnp.sum(
                left_ref[...] * right[None], axis=1, keepdims=True
            )

    for q in range(CHUNKS + 1):
        if q < CHUNKS:
            for t in range(3):
                copy(GATHER + t, q).wait_recv()
            copy(SWAP, q).start()
            contract(core, q)
        if q > 0:
            copy(SWAP, q - 1).wait_recv()
            contract(1 - core, q - 1)

    product = prod_ref[...].reshape(local_rows * width, channels)
    normed_out = layer_norm(product, out_gain_ref[...]).astype(jnp.bfloat16)
    result = jnp.dot(normed_out, w_out_ref[...], preferred_element_type=jnp.float32)
    o_ref[...] = (gate_vals * result).astype(jnp.bfloat16).reshape(local_rows, width, channels)

    for q in range(CHUNKS):
        for kind in range(SWAP + 1):
            copy(kind, q).wait_send()


def fused(
    pair_rows, in_gain, w_left, w_left_gate, w_right, w_right_gate, w_gate, w_out, out_gain, valid_len, window
):
    local_rows, tokens, channels = pair_rows.shape
    width = tokens // 8
    vmem = pl.BlockSpec(memory_space=pltpu.VMEM)
    smem = pl.BlockSpec(memory_space=pltpu.SMEM)
    part = (local_rows, tokens // QUAD, channels)
    return pl.pallas_call(
        fused_kernel,
        out_shape=jax.ShapeDtypeStruct((local_rows, width, channels), jnp.bfloat16),
        in_specs=[smem, smem] + [pl.BlockSpec(memory_space=pl.ANY)] * 9,
        out_specs=vmem,
        scratch_shapes=[
            pltpu.VMEM((local_rows, tokens, channels), jnp.bfloat16),
            pltpu.VMEM((1, channels), jnp.float32),
            *[pltpu.VMEM((channels, channels), jnp.bfloat16)] * 6,
            pltpu.VMEM((1, channels), jnp.float32),
            pltpu.VMEM((local_rows, tokens, channels), jnp.bfloat16),
            pltpu.VMEM((local_rows, tokens, channels), jnp.float32),
            pltpu.VMEM((3, *part), jnp.bfloat16),
            pltpu.VMEM(part, jnp.bfloat16),
            pltpu.VMEM(part, jnp.bfloat16),
            pltpu.VMEM((2, local_rows, tokens, channels), jnp.bfloat16),
            pltpu.VMEM((local_rows, width, channels), jnp.float32),
            pltpu.SemaphoreType.DMA((SWAP + 1, CHUNKS)),
            pltpu.SemaphoreType.DMA((SWAP + 1, CHUNKS)),
            pltpu.SemaphoreType.DMA((8 + CHUNKS,)),
        ],
        compiler_params=pltpu.CompilerParams(collective_id=0, has_side_effects=True),
    )(
        valid_len,
        window,
        pair_rows,
        in_gain.reshape(1, channels),
        w_left,
        w_left_gate,
        w_right,
        w_right_gate,
        w_gate,
        w_out,
        out_gain.reshape(1, channels),
    )


def on_device_any(row_devices, pair_rows, *rest):
    local_rows, tokens, channels = pair_rows.shape
    fits = row_devices == QUAD * 4 and tokens // 8 == 2 * local_rows and local_rows % CHUNKS == 0
    return (fused if fits else on_device)(pair_rows, *rest)


def solution(mesh):
    return jax.shard_map(
        functools.partial(on_device_any, mesh.shape["row"]),
        mesh=mesh,
        in_specs=(
            P(("groups", "row"), None, None),
            P(),
            P(),
            P(),
            P(),
            P(),
            P(),
            P(),
            P(),
            P("groups"),
            P("groups"),
        ),
        out_specs=P(("groups", "row"), None, None),
        check_vma=False,
    )
```
